32 devices in a mesh: groups: 2 (over x), seq: 16 (over z, y, core).
Axes of the slice: x: 2, y: 2, z: 4, core: 2. Of those that a mesh axis runs over, the one named last changes fastest.
Arguments:
- hidden: bfloat16 [16384, 4096], P(('groups', 'seq')), parts along dimension 0, may hold values from -6 to 6
- norm_gain: bfloat16 [4096], replicated, may hold values from 0.5 to 1.5
- w_query: bfloat16 [4096, 32], replicated, may hold values from -0.09375 to 0.09375
- w_key: bfloat16 [4096, 32], replicated, may hold values from -0.09375 to 0.09375
- conv_kernel: float32 [4, 32], replicated, may hold values from -3 to 3
- out_gain: bfloat16 [4096], replicated, may hold values from 0.5 to 1.5
Outputs:
- adapted: bfloat16 [16384, 4096], P(('groups', 'seq')), parts along dimension 0
The draws below stay inside these ranges and needn't reach their ends.
There are 2 independent parts, one for each index of `groups`. The reference program is written for one: setup_inputs(seed, part) draws one part's arguments, and reference() takes and returns one part's arrays. A program takes and returns all parts, laid end to end along the dimension named above; an argument that names none is the same for every part. Nothing has to cross between parts.
All inputs are finite; a program needn't handle non-finite values.
Results may differ from the reference program's by a relative error of at most 0.0097.
Values may be sent and summed in bfloat16 or wider, within the bound.
A program may use at most 128 MiB of HBM per device.

```python
import jax
import jax.numpy as jnp
from jax import lax

D = 4096
R = 32
CONV = 4
TOK_DEV = 512
TOKENS = 8192


def level_of(key, extent, split, low, largest):
    def one(axis_at, parts):
        steps = jax.random.uniform(jax.random.fold_in(jax.random.fold_in(key, 6), axis_at), (parts,), jnp.float32, low / len(split), largest / len(split))
        return jnp.repeat(jnp.exp(steps), extent[axis_at] // parts).reshape((-1,) + (1,) * (len(extent) - axis_at - 1))

    loudness = one(*split[0])
    for cut in split[1:]:
        loudness = loudness * one(*cut)
    return loudness


def noise(rng, shape, scale, limit, split=(), kind=jnp.bfloat16):
    drawn = scale * jax.random.normal(rng, shape, jnp.float32)
    if split:
        drawn = drawn * level_of(rng, shape, split, -0.22, 0.18)
    return jnp.clip(drawn, -limit, limit).astype(kind)


def setup_inputs(seed: int = 0, part: int = 0) -> dict:
    key_list = jax.random.split(jax.random.key(seed), 7)
    part_keys = jax.random.split(jax.random.fold_in(key_list[6], part), 7)
    hidden = noise(part_keys[0], (TOKENS, D), 1.0, 6.0, ((0, 16),))
    norm_gain = jnp.clip(1.0 + 0.1 * jax.random.normal(key_list[1], (D,), jnp.float32), 0.5, 1.5).astype(jnp.bfloat16)
    w_query = noise(key_list[2], (D, R), D ** -0.5, 0.09375)
    w_key = noise(key_list[3], (D, R), D ** -0.5, 0.09375)
    conv_kernel = noise(key_list[4], (CONV, R), 0.5, 3.0, (), jnp.float32)
    out_gain = jnp.clip(1.0 + 0.1 * jax.random.normal(key_list[5], (D,), jnp.float32), 0.5, 1.5).astype(jnp.bfloat16)
    return {"hidden": hidden, "norm_gain": norm_gain, "w_query": w_query, "w_key": w_key, "conv_kernel": conv_kernel, "out_gain": out_gain}


epsilon = 1e-06

def rms_scale(values, gain):
    floats = values.astype(jnp.float32)
    inv_rms = lax.rsqrt(lax.optimization_barrier(jnp.mean(floats * floats, axis=-1, keepdims=True)) + epsilon)
    return floats * inv_rms * gain.astype(jnp.float32)

def reference(hidden, norm_gain, w_query, w_key, conv_kernel, out_gain):
    normed = rms_scale(hidden, norm_gain).astype(jnp.bfloat16)
    queries = jnp.dot(normed, w_query, preferred_element_type=jnp.float32).astype(jnp.bfloat16)
    raw_keys = jnp.dot(normed, w_key, preferred_element_type=jnp.float32).astype(jnp.bfloat16)
    width = conv_kernel.shape[0]
    padded = jnp.concatenate([jnp.zeros((width - 1, R), raw_keys.dtype), raw_keys], axis=0)
    summed = jnp.zeros((TOKENS, R), jnp.float32)
    for offset in range(width):
        start = width - 1 - offset
        summed = summed + conv_kernel[offset][None, :] * padded[start:start + TOKENS].astype(jnp.float32)
    key_rows = summed.astype(jnp.bfloat16)
    slabs = TOKENS // TOK_DEV
    hid_slabs = hidden.reshape(slabs, TOK_DEV, D)
    key_slabs = key_rows.reshape(slabs, TOK_DEV, R)
    query_slabs = queries.reshape(slabs, TOK_DEV, R)

    def slab_state(items):
        return lax.dot_general(items[1], items[0], (((0,), (0,)), ((), ())), preferred_element_type=jnp.float32)
    states = lax.map(slab_state, (hid_slabs, key_slabs))
    running = jnp.cumsum(states, axis=0)[:-1]
    prefix_state = jnp.concatenate([jnp.zeros((1, R, D), jnp.float32), running], axis=0)
    positions = jnp.arange(TOK_DEV, dtype=jnp.int32)
    causal = positions[:, None] >= positions[None, :]

    def one_slab(items):
        query_rows, slab_keys, slab_hidden, prefix = items
        prefix_low = prefix.astype(jnp.bfloat16)
        carried = jnp.dot(query_rows, prefix_low, preferred_element_type=jnp.float32)
        scores = lax.dot_general(query_rows, slab_keys, (((1,), (1,)), ((), ())), preferred_element_type=jnp.float32)
        scores = jnp.where(causal, scores, jnp.zeros_like(scores)).astype(jnp.bfloat16)
        local_term = jnp.dot(scores, slab_hidden, preferred_element_type=jnp.float32)
        mixed = carried + local_term
        return rms_scale(mixed, out_gain).astype(jnp.bfloat16)
    adapted = lax.map(one_slab, (query_slabs, key_slabs, hid_slabs, prefix_state))
    return adapted.reshape(TOKENS, D)
```

```python
import functools

import jax
import jax.numpy as jnp
from jax import lax
from jax.experimental import pallas as pl
from jax.experimental.pallas import tpu as pltpu
from jax.sharding import PartitionSpec as P

epsilon = 1e-06
MESH = pl.DeviceIdType.MESH
F32 = jnp.float32
BF16 = jnp.bfloat16


def state_kernel(n, team, hidden, gain, w_key, w_query, conv, local_out, q_out, pref_out,
                 hbuf, wcat, rk, tail, halo, kbuf, qbuf, sbuf, own, got, total, got2, acc, pbuf,
                 load_sem, halo_sem, send1, recv1, send2, recv2, send3, recv3):
    rows, width = hbuf.shape
    rank = w_key.shape[0]
    taps = conv.shape[0]
    part = width // team
    planes = n // team
    chunks = load_sem.shape[0]
    step = rows // chunks
    me = lax.axis_index("seq")
    pos = lax.rem(me, team)
    plane = me // team
    order = [chunks - 1] + list(range(chunks - 1))

    def load(c):
        span = pl.ds(c * step, step)
        return pltpu.make_async_copy(hidden.at[span], hbuf.at[span], load_sem.at[c])

    for c in order:
        load(c).start()

    barrier = pltpu.get_barrier_semaphore()

    def greet(other):
        pl.semaphore_signal(barrier, inc=1, device_id={"seq": other}, device_id_type=MESH)

    for j in range(1, n):
        greet(lax.rem(me + j, n))

    scale = gain[...].astype(F32).reshape(1, width)
    wcat[pl.ds(0, rank), :] = (w_key[...].astype(F32) * scale).astype(BF16)
    wcat[pl.ds(rank, rank), :] = (w_query[...].astype(F32) * scale).astype(BF16)
    halo_copy = pltpu.make_async_remote_copy(
        src_ref=tail, dst_ref=halo, send_sem=halo_sem.at[0], recv_sem=halo_sem.at[1],
        device_id={"seq": jnp.minimum(me + 1, n - 1)}, device_id_type=MESH)

    for c in order:
        load(c).wait()
        h = hbuf[pl.ds(c * step, step), :]
        hf = h.astype(F32)
        inv = lax.rsqrt(jnp.sum(hf * hf, axis=1, keepdims=True) * (1.0 / width) + epsilon)
        proj = lax.dot_general(h, wcat[...], (((1,), (1,)), ((), ())), preferred_element_type=F32)
        proj = (proj * inv).astype(BF16)
        qbuf[pl.ds(c * step, step), :] = proj[:, rank:]
        keys = proj[:, :rank].astype(F32)
        rk[pl.ds(8 + c * step, step), :] = keys
        if c == chunks - 1:
            tail[:, :rank] = keys[step - 8:, :]
            tail[:, rank:] = jnp.zeros((8, tail.shape[1] - rank), F32)
            pl.semaphore_wait(barrier, n - 1)

            @pl.when(me < n - 1)
            def _():
                halo_copy.start()

    @pl.when(me > 0)
    def _():
        halo_copy.wait_recv()
        rk[pl.ds(0, 8), :] = halo[:, :rank]

    @pl.when(me == 0)
    def _():
        rk[pl.ds(0, 8), :] = jnp.zeros((8, rank), F32)

    summed = conv[0:1, :] * rk[pl.ds(8, rows), :]
    for j in range(1, taps):
        summed = summed + conv[j:j + 1, :] * rk[pl.ds(8 - j, rows), :]
    kbuf[...] = summed.astype(BF16)
    keys_t = summed.T.astype(BF16)

    for p in range(team):
        own[p] = jnp.dot(keys_t, hbuf[:, p * part:(p + 1) * part], preferred_element_type=F32).astype(BF16)

    def phase1(j):
        to = lax.rem(pos + j, team)
        return pltpu.make_async_remote_copy(
            src_ref=own.at[to], dst_ref=got.at[pos], send_sem=send1.at[j - 1], recv_sem=recv1.at[j - 1],
            device_id={"seq": plane * team + to}, device_id_type=MESH)

    def phase2(k):
        return pltpu.make_async_remote_copy(
            src_ref=total, dst_ref=got2.at[k - 1], send_sem=send2.at[k - 1], recv_sem=recv2.at[k - 1],
            device_id={"seq": lax.rem(plane + k, planes) * team + pos}, device_id_type=MESH)

    def phase3(j):
        to = lax.rem(pos + j, team)
        return pltpu.make_async_remote_copy(
            src_ref=pbuf.at[to], dst_ref=pref_out.at[pos], send_sem=send3.at[j - 1], recv_sem=recv3.at[j - 1],
            device_id={"seq": plane * team + to}, device_id_type=MESH)

    for j in range(1, team):
        phase1(j).start()
    got[pos] = own[pos]

    q = qbuf[...]
    q_out[...] = q
    scores = lax.dot_general(q, kbuf[...], (((1,), (1,)), ((), ())), preferred_element_type=F32)
    at_row = lax.broadcasted_iota(jnp.int32, scores.shape, 0)
    at_col = lax.broadcasted_iota(jnp.int32, scores.shape, 1)
    sbuf[...] = jnp.where(at_row >= at_col, scores, 0.0).astype(BF16)

    halves = 2
    half = rows // halves
    tile = 512

    def local(b):
        depth = (b + 1) * half

        @pl.loop(0, width // tile)
        def _(t):
            cols = pl.ds(pl.multiple_of(t * tile, tile), tile)
            local_out[pl.ds(b * half, half), cols] = jnp.dot(
                sbuf[pl.ds(b * half, half), pl.ds(0, depth)], hbuf[pl.ds(0, depth), cols],
                preferred_element_type=F32)

    local(0)

    for j in range(1, team):
        phase1(j).wait()
    total[...] = sum(got[p].astype(F32) for p in range(team)).astype(BF16)
    for k in range(1, planes):
        @pl.when(plane + k < planes)
        def _():
            phase2(k).start()

    local(1)

    acc[...] = jnp.zeros_like(acc)
    for k in range(1, planes):
        @pl.when(plane >= k)
        def _():
            phase2(k).wait_recv()
            acc[...] += got2[k - 1].astype(F32)

    running = acc[...]
    for p in range(team):
        pbuf[p] = running.astype(BF16)
        if p < team - 1:
            running = running + got[p].astype(F32)
    for j in range(1, team):
        phase3(j).start()
    pref_out[pos] = pbuf[pos]
    for j in range(1, team):
        phase3(j).wait()
    for k in range(1, planes):
        @pl.when(plane + k < planes)
        def _():
            phase2(k).wait_send()

    @pl.when(me < n - 1)
    def _():
        halo_copy.wait_send()


def finish_kernel(local, q, pref, gain, out, mixed, done, sem):
    team, _, part = pref.shape
    width = team * part
    blocks = sem.shape[0]
    block = local.shape[0] // blocks
    scale = gain[...].astype(F32).reshape(1, width)
    copies = []
    for b in range(blocks):
        span = pl.ds(b * block, block)
        squares = jnp.zeros((block, 1), F32)
        for p in range(team):
            cols = pl.ds(p * part, part)
            m = local[span, cols] + jnp.dot(q[span, :], pref[p], preferred_element_type=F32)
            mixed[:, cols] = m
            squares = squares + jnp.sum(m * m, axis=1, keepdims=True)
        inv = lax.rsqrt(squares * (1.0 / width) + epsilon)
        done[span, :] = (mixed[...] * inv * scale).astype(BF16)
        copies.append(pltpu.make_async_copy(done.at[span], out.at[span], sem.at[b]))
        copies[-1].start()
    for copy in copies:
        copy.wait()


def shards(n, hidden, norm_gain, w_query, w_key, conv_kernel, out_gain):
    rows, width = hidden.shape
    taps, rank = conv_kernel.shape
    team = 4
    planes = n // team
    part = width // team
    chunks = 4
    vmem = pl.BlockSpec(memory_space=pltpu.VMEM)
    anyspace = pl.BlockSpec(memory_space=pltpu.HBM)
    dma = pltpu.SemaphoreType.DMA
    later = max(planes - 1, 1)
    local, q, pref = pl.pallas_call(
        functools.partial(state_kernel, n, team),
        out_shape=(jax.ShapeDtypeStruct((rows, width), F32),
                   jax.ShapeDtypeStruct((rows, rank), BF16),
                   jax.ShapeDtypeStruct((team, rank, part), BF16)),
        in_specs=[anyspace, vmem, vmem, vmem, vmem],
        out_specs=(vmem, vmem, vmem),
        scratch_shapes=[
            pltpu.VMEM((rows, width), BF16),
            pltpu.VMEM((2 * rank, width), BF16),
            pltpu.VMEM((rows + 8, rank), F32),
            pltpu.VMEM((8, 128), F32),
            pltpu.VMEM((8, 128), F32),
            pltpu.VMEM((rows, rank), BF16),
            pltpu.VMEM((rows, rank), BF16),
            pltpu.VMEM((rows, rows), BF16),
            pltpu.VMEM((team, rank, part), BF16),
            pltpu.VMEM((team, rank, part), BF16),
            pltpu.VMEM((rank, part), BF16),
            pltpu.VMEM((later, rank, part), BF16),
            pltpu.VMEM((rank, part), F32),
            pltpu.VMEM((team, rank, part), BF16),
            dma((chunks,)), dma((2,)),
            dma((team - 1,)), dma((team - 1,)),
            dma((later,)), dma((later,)),
            dma((team - 1,)), dma((team - 1,)),
        ],
        compiler_params=pltpu.CompilerParams(
            collective_id=0, has_side_effects=True, vmem_limit_bytes=32 * 1024 * 1024),
    )(hidden, norm_gain, w_key.T, w_query.T, conv_kernel)

    return pl.pallas_call(
        finish_kernel,
        out_shape=jax.ShapeDtypeStruct((rows, width), BF16),
        in_specs=[vmem, vmem, vmem, vmem],
        out_specs=anyspace,
        scratch_shapes=[pltpu.VMEM((rows // 8, width), F32), pltpu.VMEM((rows, width), BF16), dma((8,))],
        compiler_params=pltpu.CompilerParams(vmem_limit_bytes=32 * 1024 * 1024),
    )(local, q, pref, out_gain)


def solution(mesh):
    placed = (P(("groups", "seq"), None), P(), P(), P(), P(), P())
    return jax.shard_map(
        functools.partial(shards, mesh.shape["seq"]), mesh=mesh, in_specs=placed,
        out_specs=P(("groups", "seq"), None), check_vma=False
    )
```

```python
import functools

import jax
import jax.numpy as jnp
from jax import lax
from jax.experimental import pallas as pl
from jax.experimental.pallas import tpu as pltpu
from jax.sharding import PartitionSpec as P

epsilon = 1e-06
MESH = pl.DeviceIdType.MESH
F32 = jnp.float32
BF16 = jnp.bfloat16


def state_kernel(n, team, pieces, hidden, gain_in, w_key_in, w_query_in, conv_in, local_out, q_out, pref_out,
                 hbuf, gain, w_key, w_query, conv, wcat, rk, tail, halo, kbuf, qbuf, sbuf, own, got, total, got2, acc, pbuf,
                 small_sem, load_sem, halo_sem, send1, recv1, send2, recv2, send3, recv3):
    rows, width = hbuf.shape
    rank = w_key.shape[0]
    taps = conv.shape[0]
    part = width // (team * pieces)
    planes = n // team
    chunks = load_sem.shape[0]
    step = rows // chunks
    me = lax.axis_index("seq")
    pos = lax.rem(me, team)
    plane = me // team
    order = [chunks - 1] + list(range(chunks - 1))

    def load(c):
        span = pl.ds(c * step, step)
        return pltpu.make_async_copy(hidden.at[span], hbuf.at[span], load_sem.at[c])

    small = [pltpu.make_async_copy(src, dst, small_sem.at[i]) for i, (src, dst) in enumerate(
        ((w_key_in, w_key), (w_query_in, w_query), (gain_in, gain), (conv_in, conv)))]
    for copy in small:
        copy.start()
    for c in order:
        load(c).start()

    barrier = pltpu.get_barrier_semaphore()

    def greet(other):
        pl.semaphore_signal(barrier, inc=1, device_id={"seq": other}, device_id_type=MESH)

    for j in range(1, n):
        greet(lax.rem(me + j, n))

    for copy in small:
        copy.wait()
    scale = gain[...].astype(F32).reshape(1, width)
    wcat[pl.ds(0, rank), :] = (w_key[...].astype(F32) * scale).astype(BF16)
    wcat[pl.ds(rank, rank), :] = (w_query[...].astype(F32) * scale).astype(BF16)
    halo_copy = pltpu.make_async_remote_copy(
        src_ref=tail, dst_ref=halo, send_sem=halo_sem.at[0], recv_sem=halo_sem.at[1],
        device_id={"seq": jnp.minimum(me + 1, n - 1)}, device_id_type=MESH)

    for c in order:
        load(c).wait()
        h = hbuf[pl.ds(c * step, step), :]
        hf = h.astype(F32)
        inv = lax.rsqrt(jnp.sum(hf * hf, axis=1, keepdims=True) * (1.0 / width) + epsilon)
        proj = lax.dot_general(h, wcat[...], (((1,), (1,)), ((), ())), preferred_element_type=F32)
        proj = (proj * inv).astype(BF16)
        qbuf[pl.ds(c * step, step), :] = proj[:, rank:]
        keys = proj[:, :rank].astype(F32)
        rk[pl.ds(8 + c * step, step), :] = keys
        if c == chunks - 1:
            tail[:, :rank] = keys[step - 8:, :]
            tail[:, rank:] = jnp.zeros((8, tail.shape[1] - rank), F32)
            pl.semaphore_wait(barrier, n - 1)

            @pl.when(me < n - 1)
            def _():
                halo_copy.start()

    @pl.when(me > 0)
    def _():
        halo_copy.wait_recv()
        rk[pl.ds(0, 8), :] = halo[:, :rank]

    @pl.when(me == 0)
    def _():
        rk[pl.ds(0, 8), :] = jnp.zeros((8, rank), F32)

    summed = conv[0:1, :] * rk[pl.ds(8, rows), :]
    for j in range(1, taps):
        summed = summed + conv[j:j + 1, :] * rk[pl.ds(8 - j, rows), :]
    kbuf[...] = summed.astype(BF16)
    keys_t = summed.T.astype(BF16)

    def phase1(j, c):
        to = lax.rem(pos + j, team)
        return pltpu.make_async_remote_copy(
            src_ref=own.at[to * pieces + c], dst_ref=got.at[pos * pieces + c],
            send_sem=send1.at[j - 1, c], recv_sem=recv1.at[j - 1, c],
            device_id={"seq": plane * team + to}, device_id_type=MESH)

    def phase2(k, c):
        return pltpu.make_async_remote_copy(
            src_ref=total.at[c], dst_ref=got2.at[k - 1, c],
            send_sem=send2.at[k - 1, c], recv_sem=recv2.at[k - 1, c],
            device_id={"seq": lax.rem(plane + k, planes) * team + pos}, device_id_type=MESH)

    def phase3(j, c):
        to = lax.rem(pos + j, team)
        return pltpu.make_async_remote_copy(
            src_ref=pbuf.at[to * pieces + c], dst_ref=pref_out.at[pos * pieces + c],
            send_sem=send3.at[j - 1, c], recv_sem=recv3.at[j - 1, c],
            device_id={"seq": plane * team + to}, device_id_type=MESH)

    for c in range(pieces):
        for p in range(team):
            at = p * pieces + c
            own[at] = jnp.dot(keys_t, hbuf[:, at * part:(at + 1) * part], preferred_element_type=F32).astype(BF16)
        for j in range(1, team):
            phase1(j, c).start()
        got[pos * pieces + c] = own[pos * pieces + c]

    q = qbuf[...]
    q_out[...] = q
    scores = lax.dot_general(q, kbuf[...], (((1,), (1,)), ((), ())), preferred_element_type=F32)
    at_row = lax.broadcasted_iota(jnp.int32, scores.shape, 0)
    at_col = lax.broadcasted_iota(jnp.int32, scores.shape, 1)
    sbuf[...] = jnp.where(at_row >= at_col, scores, 0.0).astype(BF16)

    halves = 2
    half = rows // halves
    tile = 512

    def local(b):
        depth = (b + 1) * half

        @pl.loop(0, width // tile)
        def _(t):
            cols = pl.ds(pl.multiple_of(t * tile, tile), tile)
            local_out[pl.ds(b * half, half), cols] = jnp.dot(
                sbuf[pl.ds(b * half, half), pl.ds(0, depth)], hbuf[pl.ds(0, depth), cols],
                preferred_element_type=F32)

    local(0)

    for c in range(pieces):
        for j in range(1, team):
            phase1(j, c).wait()
        total[c] = sum(got[p * pieces + c].astype(F32) for p in range(team)).astype(BF16)
        for k in range(1, planes):
            @pl.when(plane + k < planes)
            def _():
                phase2(k, c).start()

    local(1)

    for c in range(pieces):
        acc[...] = jnp.zeros_like(acc)
        for k in range(1, planes):
            @pl.when(plane >= k)
            def _():
                phase2(k, c).wait_recv()
                acc[...] += got2[k - 1, c].astype(F32)

        running = acc[...]
        for p in range(team):
            pbuf[p * pieces + c] = running.astype(BF16)
            if p < team - 1:
                running = running + got[p * pieces + c].astype(F32)
        for j in range(1, team):
            phase3(j, c).start()
        pref_out[pos * pieces + c] = pbuf[pos * pieces + c]

    for c in range(pieces):
        for j in range(1, team):
            phase3(j, c).wait()
        for k in range(1, planes):
            @pl.when(plane + k < planes)
            def _():
                phase2(k, c).wait_send()

    @pl.when(me < n - 1)
    def _():
        halo_copy.wait_send()


def finish_kernel(local, q, pref, gain, out, mixed, done, sem):
    team, _, part = pref.shape
    width = team * part
    blocks = sem.shape[0]
    block = local.shape[0] // blocks
    scale = gain[...].astype(F32).reshape(1, width)
    copies = []
    for b in range(blocks):
        span = pl.ds(b * block, block)
        squares = jnp.zeros((block, 1), F32)
        for p in range(team):
            cols = pl.ds(p * part, part)
            m = local[span, cols] + jnp.dot(q[span, :], pref[p], preferred_element_type=F32)
            mixed[:, cols] = m
            squares = squares + jnp.sum(m * m, axis=1, keepdims=True)
        inv = lax.rsqrt(squares * (1.0 / width) + epsilon)
        done[span, :] = (mixed[...] * inv * scale).astype(BF16)
        copies.append(pltpu.make_async_copy(done.at[span], out.at[span], sem.at[b]))
        copies[-1].start()
    for copy in copies:
        copy.wait()


def shards(n, hidden, norm_gain, w_query, w_key, conv_kernel, out_gain):
    rows, width = hidden.shape
    taps, rank = conv_kernel.shape
    team = 4
    planes = n // team
    pieces = 2
    part = width // (team * pieces)
    chunks = 4
    vmem = pl.BlockSpec(memory_space=pltpu.VMEM)
    anyspace = pl.BlockSpec(memory_space=pltpu.HBM)
    dma = pltpu.SemaphoreType.DMA
    later = max(planes - 1, 1)
    local, q, pref = pl.pallas_call(
        functools.partial(state_kernel, n, team, pieces),
        out_shape=(jax.ShapeDtypeStruct((rows, width), F32),
                   jax.ShapeDtypeStruct((rows, rank), BF16),
                   jax.ShapeDtypeStruct((team * pieces, rank, part), BF16)),
        in_specs=[anyspace] * 5,
        out_specs=(vmem, vmem, vmem),
        scratch_shapes=[
            pltpu.VMEM((rows, width), BF16),
            pltpu.VMEM((width,), BF16),
            pltpu.VMEM((rank, width), BF16),
            pltpu.VMEM((rank, width), BF16),
            pltpu.VMEM((taps, rank), F32),
            pltpu.VMEM((2 * rank, width), BF16),
            pltpu.VMEM((rows + 8, rank), F32),
            pltpu.VMEM((8, 128), F32),
            pltpu.VMEM((8, 128), F32),
            pltpu.VMEM((rows, rank), BF16),
            pltpu.VMEM((rows, rank), BF16),
            pltpu.VMEM((rows, rows), BF16),
            pltpu.VMEM((team * pieces, rank, part), BF16),
            pltpu.VMEM((team * pieces, rank, part), BF16),
            pltpu.VMEM((pieces, rank, part), BF16),
            pltpu.VMEM((later, pieces, rank, part), BF16),
            pltpu.VMEM((rank, part), F32),
            pltpu.VMEM((team * pieces, rank, part), BF16),
            dma((4,)), dma((chunks,)), dma((2,)),
            dma((team - 1, pieces)), dma((team - 1, pieces)),
            dma((later, pieces)), dma((later, pieces)),
            dma((team - 1, pieces)), dma((team - 1, pieces)),
        ],
        compiler_params=pltpu.CompilerParams(
            collective_id=0, has_side_effects=True, vmem_limit_bytes=32 * 1024 * 1024),
    )(*(pltpu.with_memory_space_constraint(x, pltpu.HBM) for x in (
        hidden, norm_gain, w_key.T, w_query.T, conv_kernel)))

    return pl.pallas_call(
        finish_kernel,
        out_shape=jax.ShapeDtypeStruct((rows, width), BF16),
        in_specs=[vmem, vmem, vmem, vmem],
        out_specs=anyspace,
        scratch_shapes=[pltpu.VMEM((rows // 8, width), F32), pltpu.VMEM((rows, width), BF16), dma((8,))],
        compiler_params=pltpu.CompilerParams(vmem_limit_bytes=32 * 1024 * 1024),
    )(local, q, pref, out_gain)


def solution(mesh):
    placed = (P(("groups", "seq"), None), P(), P(), P(), P(), P())
    return jax.shard_map(
        functools.partial(shards, mesh.shape["seq"]), mesh=mesh, in_specs=placed,
        out_specs=P(("groups", "seq"), None), check_vma=False
    )
```

```python
import functools

import jax
import jax.numpy as jnp
from jax import lax
from jax.experimental import pallas as pl
from jax.experimental.pallas import tpu as pltpu
from jax.sharding import PartitionSpec as P

epsilon = 1e-06
MESH = pl.DeviceIdType.MESH
F32 = jnp.float32
BF16 = jnp.bfloat16


def state_kernel(n, team, pieces, hidden, gain_in, w_key_in, w_query_in, conv_in, mixed, inv_out,
                 pref, squares, hbuf, gain, w_key, w_query, conv, wcat, rk, tail, halo, kbuf, qbuf, sbuf, own, got, total, got2, acc, pbuf,
                 small_sem, load_sem, halo_sem, send1, recv1, send2, recv2, send3, recv3):
    rows, width = hbuf.shape
    rank = w_key.shape[0]
    taps = conv.shape[0]
    part = width // (team * pieces)
    planes = n // team
    chunks = load_sem.shape[0]
    step = rows // chunks
    me = lax.axis_index("seq")
    pos = lax.rem(me, team)
    plane = me // team
    rounds = (planes - 1).bit_length()

    def takes(r):
        return lax.rem(plane // 2 ** r, 2) == 1

    def gives(r, k):
        return (lax.rem(plane, 2 ** (r + 1)) == 2 ** r - 1) & (plane + k < planes)

    order = [chunks - 1] + list(range(chunks - 1))

    def load(c):
        span = pl.ds(c * step, step)
        return pltpu.make_async_copy(hidden.at[span], hbuf.at[span], load_sem.at[c])

    small = [pltpu.make_async_copy(src, dst, small_sem.at[i]) for i, (src, dst) in enumerate(
        ((w_key_in, w_key), (w_query_in, w_query), (gain_in, gain), (conv_in, conv)))]
    for copy in small:
        copy.start()
    for c in order:
        load(c).start()

    barrier = pltpu.get_barrier_semaphore()

    def greet(other):
        pl.semaphore_signal(barrier, inc=1, device_id={"seq": other}, device_id_type=MESH)

    for j in range(1, team):
        greet(plane * team + lax.rem(pos + j, team))

    @pl.when((pos == 0) & (me > 0))
    def _():
        greet(me - 1)

    for r in range(rounds):
        @pl.when(takes(r))
        def _():
            greet((plane // 2 ** r * 2 ** r - 1) * team + pos)

    for copy in small:
        copy.wait()
    scale = gain[...].astype(F32).reshape(1, width)
    wcat[pl.ds(0, rank), :] = (w_key[...].astype(F32) * scale).astype(BF16)
    wcat[pl.ds(rank, rank), :] = (w_query[...].astype(F32) * scale).astype(BF16)
    halo_copy = pltpu.make_async_remote_copy(
        src_ref=tail, dst_ref=halo, send_sem=halo_sem.at[0], recv_sem=halo_sem.at[1],
        device_id={"seq": jnp.minimum(me + 1, n - 1)}, device_id_type=MESH)

    for c in order:
        load(c).wait()
        h = hbuf[pl.ds(c * step, step), :]
        hf = h.astype(F32)
        inv = lax.rsqrt(jnp.sum(hf * hf, axis=1, keepdims=True) * (1.0 / width) + epsilon)
        proj = lax.dot_general(h, wcat[...], (((1,), (1,)), ((), ())), preferred_element_type=F32)
        proj = (proj * inv).astype(BF16)
        qbuf[pl.ds(c * step, step), :] = proj[:, rank:]
        keys = proj[:, :rank].astype(F32)
        rk[pl.ds(8 + c * step, step), :] = keys
        if c == chunks - 1:
            tail[:, :rank] = keys[step - 8:, :]
            tail[:, rank:] = jnp.zeros((8, tail.shape[1] - rank), F32)
            peers = team - 1 + ((pos == team - 1) & (me < n - 1)).astype(jnp.int32)
            for r in range(rounds):
                for k in range(1, 2 ** r + 1):
                    peers = peers + gives(r, k).astype(jnp.int32)
            pl.semaphore_wait(barrier, peers)

            @pl.when(me < n - 1)
            def _():
                halo_copy.start()

    @pl.when(me > 0)
    def _():
        halo_copy.wait_recv()
        rk[pl.ds(0, 8), :] = halo[:, :rank]

    @pl.when(me == 0)
    def _():
        rk[pl.ds(0, 8), :] = jnp.zeros((8, rank), F32)

    summed = conv[0:1, :] * rk[pl.ds(8, rows), :]
    for j in range(1, taps):
        summed = summed + conv[j:j + 1, :] * rk[pl.ds(8 - j, rows), :]
    kbuf[...] = summed.astype(BF16)
    keys_t = summed.T.astype(BF16)

    def phase1(j, c):
        to = lax.rem(pos + j, team)
        return pltpu.make_async_remote_copy(
            src_ref=own.at[to * pieces + c], dst_ref=got.at[pos * pieces + c],
            send_sem=send1.at[j - 1, c], recv_sem=recv1.at[j - 1, c],
            device_id={"seq": plane * team + to}, device_id_type=MESH)

    def phase2(r, k, c):
        slot = 2 ** r - 2 + k
        return pltpu.make_async_remote_copy(
            src_ref=total.at[r, c], dst_ref=got2.at[r, c],
            send_sem=send2.at[slot, c], recv_sem=recv2.at[r, c],
            device_id={"seq": lax.rem(plane + k, planes) * team + pos}, device_id_type=MESH)

    def pass_on(r, c):
        for k in range(1, 2 ** r + 1):
            @pl.when(gives(r, k))
            def _():
                phase2(r, k, c).start()

    def phase3(j, c):
        to = lax.rem(pos + j, team)
        return pltpu.make_async_remote_copy(
            src_ref=pbuf.at[to * pieces + c], dst_ref=pref.at[pos * pieces + c],
            send_sem=send3.at[j - 1, c], recv_sem=recv3.at[j - 1, c],
            device_id={"seq": plane * team + to}, device_id_type=MESH)

    for c in range(pieces):
        for p in range(team):
            at = p * pieces + c
            own[at] = jnp.dot(keys_t, hbuf[:, at * part:(at + 1) * part], preferred_element_type=F32).astype(BF16)
        for j in range(1, team):
            phase1(j, c).start()
        got[pos * pieces + c] = own[pos * pieces + c]

    q = qbuf[...]
    scores = lax.dot_general(q, kbuf[...], (((1,), (1,)), ((), ())), preferred_element_type=F32)
    at_row = lax.broadcasted_iota(jnp.int32, scores.shape, 0)
    at_col = lax.broadcasted_iota(jnp.int32, scores.shape, 1)
    sbuf[...] = jnp.where(at_row >= at_col, scores, 0.0).astype(BF16)

    halves = 2
    half = rows // halves
    tile = 512

    def local(b, first, last):
        depth = (b + 1) * half

        @pl.loop(first, last)
        def _(t):
            cols = pl.ds(pl.multiple_of(t * tile, tile), tile)
            mixed[pl.ds(b * half, half), cols] = jnp.dot(
                sbuf[pl.ds(b * half, half), pl.ds(0, depth)], hbuf[pl.ds(0, depth), cols],
                preferred_element_type=F32)

    tiles = width // tile
    local(0, 0, tiles)
    for c in range(pieces):
        for j in range(1, team):
            phase1(j, c).wait()
        total[0, c] = sum(got[p * pieces + c].astype(F32) for p in range(team)).astype(BF16)
        pass_on(0, c)
        acc[c] = jnp.zeros(acc.shape[1:], F32)

    local(1, 0, tiles // 2)

    def send_back(c):
        running = acc[c]
        for p in range(team):
            pbuf[p * pieces + c] = running.astype(BF16)
            if p < team - 1:
                running = running + got[p * pieces + c].astype(F32)
        for j in range(1, team):
            phase3(j, c).start()
        pref[pos * pieces + c] = pbuf[pos * pieces + c]

    for r in range(rounds):
        for c in range(pieces):
            @pl.when(takes(r))
            def _():
                phase2(r, 1, c).wait_recv()
                acc[c] += got2[r, c].astype(F32)

            if r + 1 < rounds:
                total[r + 1, c] = (acc[c] + total[0, c].astype(F32)).astype(BF16)
                pass_on(r + 1, c)
            else:
                send_back(c)
        if r == 0 and rounds > 1:
            local(1, tiles // 2, tiles)
    if rounds == 0:
        for c in range(pieces):
            send_back(c)
    if rounds < 2:
        local(1, tiles // 2, tiles)

    squares[...] = jnp.zeros_like(squares)
    band = 128
    for c in range(pieces):
        for j in range(1, team):
            phase3(j, c).wait()

        @pl.loop(0, rows // band)
        def _(t):
            span = pl.ds(pl.multiple_of(t * band, band), band)
            for p in range(team):
                at = p * pieces + c
                cols = pl.ds(at * part, part)
                m = mixed[span, cols] + jnp.dot(qbuf[span, :], pref[at], preferred_element_type=F32)
                mixed[span, cols] = m
                m = m * m
                squares[span, :] += sum(m[:, i:i + 128] for i in range(0, part, 128))

    inv_out[...] = lax.rsqrt(jnp.sum(squares[...], axis=1, keepdims=True) * (1.0 / width) + epsilon)
    for c in range(pieces):
        for r in range(rounds):
            for k in range(1, 2 ** r + 1):
                @pl.when(gives(r, k))
                def _():
                    phase2(r, k, c).wait_send()

    @pl.when(me < n - 1)
    def _():
        halo_copy.wait_send()


def finish_kernel(mixed, inv, gain, out, done, sem):
    rows, width = mixed.shape
    blocks = sem.shape[0]
    block = rows // blocks
    scale = gain[...].astype(F32).reshape(1, width)
    copies = []
    for b in range(blocks):
        span = pl.ds(b * block, block)
        done[span, :] = (mixed[span, :] * inv[span, :] * scale).astype(BF16)
        copies.append(pltpu.make_async_copy(done.at[span], out.at[span], sem.at[b]))
        copies[-1].start()
    for copy in copies:
        copy.wait()


def shards(n, hidden, norm_gain, w_query, w_key, conv_kernel, out_gain):
    rows, width = hidden.shape
    taps, rank = conv_kernel.shape
    team = 4
    planes = n // team
    pieces = 2
    part = width // (team * pieces)
    chunks = 2
    vmem = pl.BlockSpec(memory_space=pltpu.VMEM)
    anyspace = pl.BlockSpec(memory_space=pltpu.HBM)
    dma = pltpu.SemaphoreType.DMA
    rounds = max((planes - 1).bit_length(), 1)
    slots = max(2 ** rounds - 1, 1)
    mixed, inv = pl.pallas_call(
        functools.partial(state_kernel, n, team, pieces),
        out_shape=(jax.ShapeDtypeStruct((rows, width), F32),
                   jax.ShapeDtypeStruct((rows, 1), F32)),
        in_specs=[anyspace] * 5,
        out_specs=(vmem, vmem),
        scratch_shapes=[
            pltpu.VMEM((team * pieces, rank, part), BF16),
            pltpu.VMEM((rows, 128), F32),
            pltpu.VMEM((rows, width), BF16),
            pltpu.VMEM((width,), BF16),
            pltpu.VMEM((rank, width), BF16),
            pltpu.VMEM((rank, width), BF16),
            pltpu.VMEM((taps, rank), F32),
            pltpu.VMEM((2 * rank, width), BF16),
            pltpu.VMEM((rows + 8, rank), F32),
            pltpu.VMEM((8, 128), F32),
            pltpu.VMEM((8, 128), F32),
            pltpu.VMEM((rows, rank), BF16),
            pltpu.VMEM((rows, rank), BF16),
            pltpu.VMEM((rows, rows), BF16),
            pltpu.VMEM((team * pieces, rank, part), BF16),
            pltpu.VMEM((team * pieces, rank, part), BF16),
            pltpu.VMEM((rounds, pieces, rank, part), BF16),
            pltpu.VMEM((rounds, pieces, rank, part), BF16),
            pltpu.VMEM((pieces, rank, part), F32),
            pltpu.VMEM((team * pieces, rank, part), BF16),
            dma((4,)), dma((chunks,)), dma((2,)),
            dma((team - 1, pieces)), dma((team - 1, pieces)),
            dma((slots, pieces)), dma((rounds, pieces)),
            dma((team - 1, pieces)), dma((team - 1, pieces)),
        ],
        compiler_params=pltpu.CompilerParams(
            collective_id=0, has_side_effects=True, vmem_limit_bytes=32 * 1024 * 1024),
    )(*(pltpu.with_memory_space_constraint(x, pltpu.HBM) for x in (
        hidden, norm_gain, w_key.T, w_query.T, conv_kernel)))

    return pl.pallas_call(
        finish_kernel,
        out_shape=jax.ShapeDtypeStruct((rows, width), BF16),
        in_specs=[vmem, vmem, vmem],
        out_specs=anyspace,
        scratch_shapes=[pltpu.VMEM((rows, width), BF16), dma((8,))],
        compiler_params=pltpu.CompilerParams(vmem_limit_bytes=32 * 1024 * 1024),
    )(mixed, inv, out_gain)


def solution(mesh):
    placed = (P(("groups", "seq"), None), P(), P(), P(), P(), P())
    return jax.shard_map(
        functools.partial(shards, mesh.shape["seq"]), mesh=mesh, in_specs=placed,
        out_specs=P(("groups", "seq"), None), check_vma=False
    )
```

```python
import functools

import jax
import jax.numpy as jnp
from jax import lax
from jax.experimental import pallas as pl
from jax.experimental.pallas import tpu as pltpu
from jax.sharding import PartitionSpec as P

epsilon = 1e-06
MESH = pl.DeviceIdType.MESH
F32 = jnp.float32
BF16 = jnp.bfloat16


def state_kernel(n, team, pieces, hidden, gain_in, w_key_in, w_query_in, conv_in, mixed, inv_out,
                 pref, squares, hbuf, gain, w_key, w_query, conv, wcat, rk, tail, halo, kbuf, qbuf, sbuf, own, got, total, got2, acc, pbuf,
                 small_sem, load_sem, halo_sem, send1, recv1, send2, recv2, send3, recv3):
    rows, width = hbuf.shape
    rank = w_key.shape[0]
    taps = conv.shape[0]
    part = width // (team * pieces)
    planes = n // team
    chunks = load_sem.shape[0]
    step = rows // chunks
    me = lax.axis_index("seq")
    pos = lax.rem(me, team)
    plane = me // team
    rounds = (planes - 1).bit_length()

    def takes(r):
        return lax.rem(plane // 2 ** r, 2) == 1

    def gives(r, k):
        return (lax.rem(plane, 2 ** (r + 1)) == 2 ** r - 1) & (plane + k < planes)

    order = [chunks - 1] + list(range(chunks - 1))

    def load(c):
        span = pl.ds(c * step, step)
        return pltpu.make_async_copy(hidden.at[span], hbuf.at[span], load_sem.at[c])

    small = [pltpu.make_async_copy(src, dst, small_sem.at[i]) for i, (src, dst) in enumerate(
        ((w_key_in, w_key), (w_query_in, w_query), (gain_in, gain), (conv_in, conv)))]
    for copy in small:
        copy.start()
    for c in order:
        load(c).start()

    barrier = pltpu.get_barrier_semaphore()

    def greet(other):
        pl.semaphore_signal(barrier, inc=1, device_id={"seq": other}, device_id_type=MESH)

    for j in range(1, team):
        greet(plane * team + lax.rem(pos + j, team))

    @pl.when((pos == 0) & (me > 0))
    def _():
        greet(me - 1)

    for r in range(rounds):
        @pl.when(takes(r))
        def _():
            greet((plane // 2 ** r * 2 ** r - 1) * team + pos)

    for copy in small:
        copy.wait()
    scale = gain[...].astype(F32).reshape(1, width)
    wcat[pl.ds(0, rank), :] = (w_key[...].astype(F32) * scale).astype(BF16)
    wcat[pl.ds(rank, rank), :] = (w_query[...].astype(F32) * scale).astype(BF16)
    halo_copy = pltpu.make_async_remote_copy(
        src_ref=tail, dst_ref=halo, send_sem=halo_sem.at[0], recv_sem=halo_sem.at[1],
        device_id={"seq": jnp.minimum(me + 1, n - 1)}, device_id_type=MESH)

    for c in order:
        load(c).wait()
        h = hbuf[pl.ds(c * step, step), :]
        hf = h.astype(F32)
        inv = lax.rsqrt(jnp.sum(hf * hf, axis=1, keepdims=True) * (1.0 / width) + epsilon)
        proj = lax.dot_general(h, wcat[...], (((1,), (1,)), ((), ())), preferred_element_type=F32)
        proj = (proj * inv).astype(BF16)
        qbuf[pl.ds(c * step, step), :] = proj[:, rank:]
        keys = proj[:, :rank].astype(F32)
        rk[pl.ds(8 + c * step, step), :] = keys
        if c == chunks - 1:
            tail[:, :rank] = keys[step - 8:, :]
            tail[:, rank:] = jnp.zeros((8, tail.shape[1] - rank), F32)
            peers = team - 1 + ((pos == team - 1) & (me < n - 1)).astype(jnp.int32)
            for r in range(rounds):
                for k in range(1, 2 ** r + 1):
                    peers = peers + gives(r, k).astype(jnp.int32)
            pl.semaphore_wait(barrier, peers)

            @pl.when(me < n - 1)
            def _():
                halo_copy.start()

    @pl.when(me > 0)
    def _():
        halo_copy.wait_recv()
        rk[pl.ds(0, 8), :] = halo[:, :rank]

    @pl.when(me == 0)
    def _():
        rk[pl.ds(0, 8), :] = jnp.zeros((8, rank), F32)

    summed = conv[0:1, :] * rk[pl.ds(8, rows), :]
    for j in range(1, taps):
        summed = summed + conv[j:j + 1, :] * rk[pl.ds(8 - j, rows), :]
    kbuf[...] = summed.astype(BF16)
    keys_t = summed.T.astype(BF16)

    def phase1(j, c):
        to = lax.rem(pos + j, team)
        return pltpu.make_async_remote_copy(
            src_ref=own.at[to * pieces + c], dst_ref=got.at[pos * pieces + c],
            send_sem=send1.at[j - 1, c], recv_sem=recv1.at[j - 1, c],
            device_id={"seq": plane * team + to}, device_id_type=MESH)

    def phase2(r, k, c):
        slot = 2 ** r - 2 + k
        return pltpu.make_async_remote_copy(
            src_ref=total.at[r, c], dst_ref=got2.at[r, c],
            send_sem=send2.at[slot, c], recv_sem=recv2.at[r, c],
            device_id={"seq": lax.rem(plane + k, planes) * team + pos}, device_id_type=MESH)

    def pass_on(r, c):
        for k in range(1, 2 ** r + 1):
            @pl.when(gives(r, k))
            def _():
                phase2(r, k, c).start()

    def phase3(j, c):
        to = lax.rem(pos + j, team)
        return pltpu.make_async_remote_copy(
            src_ref=pbuf.at[to * pieces + c], dst_ref=pref.at[pos * pieces + c],
            send_sem=send3.at[j - 1, c], recv_sem=recv3.at[j - 1, c],
            device_id={"seq": plane * team + to}, device_id_type=MESH)

    for c in range(pieces):
        for p in range(team):
            at = p * pieces + c
            own[at] = jnp.dot(keys_t, hbuf[:, at * part:(at + 1) * part], preferred_element_type=F32).astype(BF16)
        for j in range(1, team):
            phase1(j, c).start()
        got[pos * pieces + c] = own[pos * pieces + c]

    q = qbuf[...]
    scores = lax.dot_general(q, kbuf[...], (((1,), (1,)), ((), ())), preferred_element_type=F32)
    at_row = lax.broadcasted_iota(jnp.int32, scores.shape, 0)
    at_col = lax.broadcasted_iota(jnp.int32, scores.shape, 1)
    sbuf[...] = jnp.where(at_row >= at_col, scores, 0.0).astype(BF16)

    halves = 2
    half = rows // halves
    tile = 512

    def local(b, first, last):
        depth = (b + 1) * half

        @pl.loop(first, last)
        def _(t):
            cols = pl.ds(pl.multiple_of(t * tile, tile), tile)
            mixed[pl.ds(b * half, half), cols] = jnp.dot(
                sbuf[pl.ds(b * half, half), pl.ds(0, depth)], hbuf[pl.ds(0, depth), cols],
                preferred_element_type=F32)

    tiles = width // tile
    local(0, 0, tiles)
    for c in range(pieces):
        for j in range(1, team):
            phase1(j, c).wait()
        total[0, c] = sum(got[p * pieces + c].astype(F32) for p in range(team)).astype(BF16)
        pass_on(0, c)
        acc[c] = jnp.zeros(acc.shape[1:], F32)

    local(1, 0, tiles // 2)

    def send_back(c):
        running = acc[c]
        for p in range(team):
            pbuf[p * pieces + c] = running.astype(BF16)
            if p < team - 1:
                running = running + got[p * pieces + c].astype(F32)
        for j in range(1, team):
            phase3(j, c).start()
        pref[pos * pieces + c] = pbuf[pos * pieces + c]

    for r in range(rounds):
        for c in range(pieces):
            @pl.when(takes(r))
            def _():
                phase2(r, 1, c).wait_recv()
                acc[c] += got2[r, c].astype(F32)

            if r + 1 < rounds:
                total[r + 1, c] = (acc[c] + total[0, c].astype(F32)).astype(BF16)
                pass_on(r + 1, c)
            else:
                send_back(c)
        if r == 0 and rounds > 1:
            local(1, tiles // 2, tiles)
    if rounds == 0:
        for c in range(pieces):
            send_back(c)
    if rounds < 2:
        local(1, tiles // 2, tiles)

    squares[...] = jnp.zeros_like(squares)
    band = 256
    for c in range(pieces):
        for j in range(1, team):
            phase3(j, c).wait()

        @pl.loop(0, rows // band)
        def _(t):
            span = pl.ds(pl.multiple_of(t * band, band), band)
            for p in range(team):
                at = p * pieces + c
                cols = pl.ds(at * part, part)
                m = mixed[span, cols] + jnp.dot(qbuf[span, :], pref[at], preferred_element_type=F32)
                mixed[span, cols] = m
                m = m * m
                squares[span, :] += sum(m[:, i:i + 128] for i in range(0, part, 128))

    inv_out[...] = lax.rsqrt(jnp.sum(squares[...], axis=1, keepdims=True) * (1.0 / width) + epsilon)
    for c in range(pieces):
        for r in range(rounds):
            for k in range(1, 2 ** r + 1):
                @pl.when(gives(r, k))
                def _():
                    phase2(r, k, c).wait_send()

    @pl.when(me < n - 1)
    def _():
        halo_copy.wait_send()


def finish_kernel(mixed, inv, gain, out, done, sem):
    rows, width = mixed.shape
    blocks = sem.shape[0]
    block = rows // blocks
    scale = gain[...].astype(F32).reshape(1, width)
    copies = []
    for b in range(blocks):
        span = pl.ds(b * block, block)
        done[span, :] = (mixed[span, :] * inv[span, :] * scale).astype(BF16)
        copies.append(pltpu.make_async_copy(done.at[span], out.at[span], sem.at[b]))
        copies[-1].start()
    for copy in copies:
        copy.wait()


def shards(n, hidden, norm_gain, w_query, w_key, conv_kernel, out_gain):
    rows, width = hidden.shape
    taps, rank = conv_kernel.shape
    team = 4
    planes = n // team
    pieces = 2
    part = width // (team * pieces)
    chunks = 2
    vmem = pl.BlockSpec(memory_space=pltpu.VMEM)
    anyspace = pl.BlockSpec(memory_space=pltpu.HBM)
    dma = pltpu.SemaphoreType.DMA
    rounds = max((planes - 1).bit_length(), 1)
    slots = max(2 ** rounds - 1, 1)
    mixed, inv = pl.pallas_call(
        functools.partial(state_kernel, n, team, pieces),
        out_shape=(jax.ShapeDtypeStruct((rows, width), F32),
                   jax.ShapeDtypeStruct((rows, 1), F32)),
        in_specs=[anyspace] * 5,
        out_specs=(vmem, vmem),
        scratch_shapes=[
            pltpu.VMEM((team * pieces, rank, part), BF16),
            pltpu.VMEM((rows, 128), F32),
            pltpu.VMEM((rows, width), BF16),
            pltpu.VMEM((width,), BF16),
            pltpu.VMEM((rank, width), BF16),
            pltpu.VMEM((rank, width), BF16),
            pltpu.VMEM((taps, rank), F32),
            pltpu.VMEM((2 * rank, width), BF16),
            pltpu.VMEM((rows + 8, rank), F32),
            pltpu.VMEM((8, 128), F32),
            pltpu.VMEM((8, 128), F32),
            pltpu.VMEM((rows, rank), BF16),
            pltpu.VMEM((rows, rank), BF16),
            pltpu.VMEM((rows, rows), BF16),
            pltpu.VMEM((team * pieces, rank, part), BF16),
            pltpu.VMEM((team * pieces, rank, part), BF16),
            pltpu.VMEM((rounds, pieces, rank, part), BF16),
            pltpu.VMEM((rounds, pieces, rank, part), BF16),
            pltpu.VMEM((pieces, rank, part), F32),
            pltpu.VMEM((team * pieces, rank, part), BF16),
            dma((4,)), dma((chunks,)), dma((2,)),
            dma((team - 1, pieces)), dma((team - 1, pieces)),
            dma((slots, pieces)), dma((rounds, pieces)),
            dma((team - 1, pieces)), dma((team - 1, pieces)),
        ],
        compiler_params=pltpu.CompilerParams(
            collective_id=0, has_side_effects=True, vmem_limit_bytes=32 * 1024 * 1024),
    )(*(pltpu.with_memory_space_constraint(x, pltpu.HBM) for x in (
        hidden, norm_gain, w_key.T, w_query.T, conv_kernel)))

    return pl.pallas_call(
        finish_kernel,
        out_shape=jax.ShapeDtypeStruct((rows, width), BF16),
        in_specs=[vmem, vmem, vmem],
        out_specs=anyspace,
        scratch_shapes=[pltpu.VMEM((rows, width), BF16), dma((8,))],
        compiler_params=pltpu.CompilerParams(vmem_limit_bytes=32 * 1024 * 1024),
    )(mixed, inv, out_gain)


def solution(mesh):
    placed = (P(("groups", "seq"), None), P(), P(), P(), P(), P())
    return jax.shard_map(
        functools.partial(shards, mesh.shape["seq"]), mesh=mesh, in_specs=placed,
        out_specs=P(("groups", "seq"), None), check_vma=False
    )
```
